128 devices in a mesh: pb: 4 (over z_lo, core), col: 32 (over x, y, z_hi).
Axes of the slice: x: 4, y: 4, z: 4 (z_hi: 2, z_lo: 2; z = z_hi * 2 + z_lo), core: 2. Of those that a mesh axis runs over, the one named last changes fastest.
Arguments:
- queries: float32 [131072, 1024], P(('pb', 'col')), may hold values from -6 to 6
- corpus: float32 [2048, 1024], P('col'), may hold values from -6 to 6
- rotation: float32 [1024, 1024], replicated, may hold values from -0.1875 to 0.1875
- counts: int32 [32], replicated, may hold values from 1 to 64, 1024 in all
- teacher: bfloat16 [131072, 2048], P(('pb', 'col')), may hold values from -6 to 6
- shift_student: float32 [131072], P(('pb', 'col')), may hold values from 0 to 1.5
- shift_teacher: float32 [131072], P(('pb', 'col')), may hold values from 0 to 1.5
Outputs:
- grad_rotation: float32 [1024, 1024], P(('pb', 'col'))
The draws below stay inside these ranges and needn't reach their ends.
Inputs may be any that keep to these rules, and one draw needn't show every extreme that they name: The counts sum to 1024; some index of col has all 64 slots live.
All inputs are finite; a program needn't handle non-finite values.
Results may differ from the reference program's by a relative error of at most 0.0018.
Values may be sent and summed in bfloat16 or wider, within the bound.
A program may use at most 128 MiB of HBM per device.

```python
import math
import jax
import jax.numpy as jnp
import numpy as np
from jax import lax

D = 1024
QDEV = 1024
CROWS = 64
QUERIES = 131072
N = 2048
LIVE = 1024
N_COL = 32


def levels(stream_key, extent, shards, smallest, top_value):
    def one(axis_at, shards_of):
        draws = jax.random.uniform(jax.random.fold_in(jax.random.fold_in(stream_key, 6), axis_at), (shards_of,), jnp.float32, smallest / len(shards), top_value / len(shards))
        return jnp.repeat(jnp.exp(draws), extent[axis_at] // shards_of).reshape((-1,) + (1,) * (len(extent) - axis_at - 1))

    gain = one(*shards[0])
    for cut in shards[1:]:
        gain = gain * one(*cut)
    return gain


def profile(count, total, reach, skew):
    loads = [(1 << 20) // math.isqrt(grade ** skew) + 1 for grade in range(2, count + 1)]
    surplus, given = total - reach - (count - 1), [1] * (count - 1)
    while surplus > 0:
        movable = [i for i in range(count - 1) if given[i] < reach]
        pool, remaining = sum([loads[i] for i in movable]), surplus
        for i in movable:
            extra = min(reach - given[i], max(1, remaining * loads[i] // pool), surplus)
            given[i] = given[i] + extra
            surplus = surplus - extra
    return np.array([reach] + given)


def ragged(key, number_of, total, reach, slope):
    if number_of == 2:
        one = jax.random.randint(key, (), max(1, total - reach), min(reach, total - 1) + 1)
        return jnp.stack([one, total - one])
    sizes = jnp.asarray(profile(number_of, total, reach, slope), jnp.int32)
    twos = (number_of - 1) // 2
    source_of, sink = sizes[1:1 + 2 * twos:2], sizes[2:2 + 2 * twos:2]
    margin = jnp.minimum(source_of - 1, reach - sink)
    passed = jax.random.randint(jax.random.fold_in(key, 1), (twos,), 0, 1 << 20) % (margin + 1)
    sizes = sizes.at[1:1 + 2 * twos:2].set(source_of - passed).at[2:2 + 2 * twos:2].set(sink + passed)
    return sizes[jax.random.permutation(jax.random.fold_in(key, 2), number_of)]


def normal_values(stream_key, dims, spread, reach, split=(), held_as=jnp.bfloat16):
    values = jax.random.normal(stream_key, dims, jnp.float32) * spread
    if len(split) > 0:
        values = levels(stream_key, dims, split, -0.22, 0.18) * values
    return jnp.clip(values, min=-reach, max=reach).astype(held_as)


def setup_inputs(seed: int = 0) -> dict:
    arg_keys = jax.random.split(jax.random.key(seed), 8)
    queries = normal_values(arg_keys[0], (QUERIES, D), 1.0, 6.0, ((0, 128),), jnp.float32)
    corpus = normal_values(arg_keys[1], (N, D), 1.0, 6.0, ((0, 32),), jnp.float32)
    rotation = normal_values(arg_keys[2], (D, D), D ** -0.5, 0.1875, (), jnp.float32)
    counts = ragged(arg_keys[3], N_COL, LIVE, CROWS, 2).astype(jnp.int32)
    teacher = normal_values(arg_keys[4], (QUERIES, N), 1.0, 6.0, ((0, 128),))
    shift_student = jnp.clip(1.5 * jax.random.uniform(arg_keys[5], (QUERIES,), jnp.float32) ** levels(arg_keys[5], (QUERIES,), ((0, 128),), -0.2, 0.2), 0.0, 1.5)
    shift_teacher = jnp.clip(1.5 * jax.random.uniform(arg_keys[6], (QUERIES,), jnp.float32) ** levels(arg_keys[6], (QUERIES,), ((0, 128),), -0.2, 0.2), 0.0, 1.5)
    return {"queries": queries, "corpus": corpus, "rotation": rotation, "counts": counts, "teacher": teacher, "shift_student": shift_student, "shift_teacher": shift_teacher}


code_sharp = 1.0

def reference(queries, corpus, rotation, counts, teacher, shift_student, shift_teacher):
    highest = lax.Precision.HIGHEST
    factor = 2.5 / math.sqrt(D)
    slots = jnp.arange(N, dtype=jnp.int32)
    owner = slots // CROWS
    live = (slots % CROWS < counts[owner]).astype(jnp.float32)
    corpus_code = jnp.tanh(code_sharp * jnp.dot(corpus, rotation, precision=highest, preferred_element_type=jnp.float32))
    corpus_bits = corpus_code.astype(jnp.bfloat16)
    blocks = QUERIES // QDEV
    query_blocks = queries.reshape(blocks, QDEV, D)
    teacher_blocks = teacher.reshape(blocks, QDEV, N)
    student_blocks = shift_student.reshape(blocks, QDEV)
    teacher_shifts = shift_teacher.reshape(blocks, QDEV)

    def step(carry, inputs):
        grad_acc, corpus_acc = carry
        block, teach, shift_s, shift_t = inputs
        query_code = jnp.tanh(code_sharp * jnp.dot(block, rotation, precision=highest, preferred_element_type=jnp.float32))
        query_bits = query_code.astype(jnp.bfloat16)
        scores = factor * lax.dot_general(query_bits, corpus_bits, (((1,), (1,)), ((), ())), preferred_element_type=jnp.float32)
        student = jnp.exp(scores - shift_s[:, None])
        target = jnp.exp(teach.astype(jnp.float32) - shift_t[:, None])
        weights = (live[None, :] * (student - target) / LIVE).astype(jnp.bfloat16)
        query_grad = factor * jnp.dot(weights, corpus_bits, preferred_element_type=jnp.float32)
        corpus_acc = corpus_acc + factor * lax.dot_general(weights, query_bits, (((0,), (0,)), ((), ())), preferred_element_type=jnp.float32)
        local = (1.0 - query_code * query_code) * query_grad
        grad_acc = grad_acc + lax.dot_general(block, local, (((0,), (0,)), ((), ())), precision=highest, preferred_element_type=jnp.float32)
        return ((grad_acc, corpus_acc), None)
    init = (jnp.zeros((D, D), jnp.float32), jnp.zeros((N, D), jnp.float32))
    (grad_acc, corpus_grad), _ = lax.scan(step, init, (query_blocks, teacher_blocks, student_blocks, teacher_shifts))
    corpus_local = (1.0 - corpus_code * corpus_code) * corpus_grad
    grad_acc = grad_acc + lax.dot_general(corpus, corpus_local, (((0,), (0,)), ((), ())), precision=highest, preferred_element_type=jnp.float32)
    return code_sharp * grad_acc
```

```python
import functools
import math

import jax
import jax.numpy as jnp
from jax import lax
from jax.experimental import pallas as pl
from jax.experimental.pallas import tpu as pltpu
from jax.sharding import PartitionSpec as P

MESH = pl.DeviceIdType.MESH
F32 = jnp.float32
BF16 = jnp.bfloat16

RING = 4
ORDERS = ((0, 1, 2), (1, 2, 0), (2, 0, 1))
COLUMNS = ((0, 384), (384, 384), (768, 256))
COLOURS = len(ORDERS)


def split(value):
    high = value.astype(BF16)
    return high, (value - high.astype(F32)).astype(BF16)


def dot(a, b, dims):
    return lax.dot_general(a, b, (dims, ((), ())), preferred_element_type=F32)


NN = ((1,), (0,))
NT = ((1,), (1,))
TN = ((0,), (0,))


class Place:
    def __init__(self):
        pb, col = lax.axis_index("pb"), lax.axis_index("col")
        self.at = (col // 8, (col // 2) % 4, (col % 2) * 2 + pb // 2)
        self.core = pb % 2
        self.pb = pb

    def device(self, at, core):
        x, y, z = at
        return ((z % 2) * 2 + core, x * 8 + y * 2 + z // 2)

    def peer(self, axis, step):
        at = list(self.at)
        at[axis] = (at[axis] + step) % RING
        return at[axis], self.device(at, self.core)

    def partner(self):
        return self.device(self.at, 1 - self.core)


def remote(src, dst, send, recv, device):
    return pltpu.make_async_remote_copy(
        src_ref=src,
        dst_ref=dst,
        send_sem=send,
        recv_sem=recv,
        device_id=device,
        device_id_type=MESH,
    )


class Gather:
    def __init__(self, place, codes, send, recv, pair_send, pair_recv):
        self.place, self.codes = place, codes
        self.send, self.recv = send, recv
        self.pair_send, self.pair_recv = pair_send, pair_recv

    def region(self, colour, known, last=None):
        order, (start, width) = ORDERS[colour], COLUMNS[colour]
        index = list(self.place.at)
        for axis in order[:known]:
            index[axis] = slice(None)
        if last is not None:
            index[order[2]] = last
        return self.codes.at[
            index[0], index[1], index[2], self.place.core, :, start : start + width
        ]

    def copies(self, stage):
        for colour in range(COLOURS):
            part = self.region(colour, stage)
            for step in range(1, RING):
                slot = (colour * 3 + stage) * 3 + step - 1
                _, device = self.place.peer(ORDERS[colour][stage], step)
                yield remote(
                    part, part, self.send.at[slot], self.recv.at[slot], device
                )

    def start(self, stage):
        for copy in self.copies(stage):
            copy.start()

    def wait(self, stage):
        for copy in self.copies(stage):
            copy.wait()

    def pair(self, colour, step):
        source, _ = self.place.peer(ORDERS[colour][2], -step)
        part = self.region(colour, 2, source)
        slot = colour * RING + step
        return remote(
            part,
            part,
            self.pair_send.at[slot],
            self.pair_recv.at[slot],
            self.place.partner(),
        )

    def finish(self):
        for step in range(1, RING):
            for colour in range(COLOURS):
                slot = (colour * 3 + 2) * 3 + step - 1
                part = self.region(colour, 2)
                _, device = self.place.peer(ORDERS[colour][2], step)
                remote(
                    part, part, self.send.at[slot], self.recv.at[slot], device
                ).wait()
                self.pair(colour, step).start()
        for colour in range(COLOURS):
            for step in range(RING):
                self.pair(colour, step).wait()


class Scatter:
    def __init__(self, place, total, lands, send, recv):
        self.place, self.total, self.lands = place, total, lands
        self.send, self.recv = send, recv

    def copies(self, stage):
        for colour in range(COLOURS):
            order, (start, width) = ORDERS[colour], COLUMNS[colour]
            for step in range(1, RING):
                slot = (colour * 3 + stage) * 3 + step - 1
                index = [slice(None)] * 3
                for axis in order[:stage]:
                    index[axis] = self.place.at[axis]
                index[order[stage]], device = self.place.peer(order[stage], step)
                yield remote(
                    self.total.at[index[0], index[1], index[2], :, start : start + width],
                    self.lands[stage][colour].at[step - 1],
                    self.send.at[slot],
                    self.recv.at[slot],
                    device,
                )

    def start(self, stage):
        for copy in self.copies(stage):
            copy.start()

    def wait(self, stage):
        for copy in self.copies(stage):
            copy.wait()
        for colour in range(COLOURS):
            order, (start, width) = ORDERS[colour], COLUMNS[colour]
            land = self.lands[stage][colour]
            rest = sorted(order[stage + 1 :])

            def add(item, _):
                index = list(self.place.at)
                inner = [item // RING, item % RING][2 - len(rest) :]
                for axis, at in zip(rest, inner):
                    index[axis] = at
                value = self.total[
                    index[0], index[1], index[2], :, start : start + width
                ]
                for step in range(RING - 1):
                    value = value + land[(step, *inner)]
                self.total[index[0], index[1], index[2], :, start : start + width] = value
                return 0

            lax.fori_loop(0, RING ** len(rest), add, 0)


def kernel(
    factor,
    live_total,
    q_hbm,
    c_hbm,
    r_hbm,
    counts,
    t_hbm,
    shift_s_ref,
    shift_t_ref,
    out_ref,
    big_a,
    big_b,
    t_buf,
    c_buf,
    m_hi,
    m_lo,
    q_hi,
    q_lo,
    q_bits,
    d_q,
    d_c,
    codes,
    weights,
    shift_s,
    shift_t,
    total_c,
    total_g,
    *rest,
):
    lands_c, rest = (rest[0:3], rest[3:6], rest[6:9]), rest[9:]
    lands_g, rest = (rest[0:3], rest[3:6], rest[6:9]), rest[9:]
    (
        load,
        ag_send,
        ag_recv,
        agp_send,
        agp_recv,
        c_send,
        c_recv,
        cp_send,
        cp_recv,
        g_send,
        g_recv,
        gp_send,
        gp_recv,
    ) = rest

    place = Place()
    core = place.core
    mx, my, mz = place.at

    load_r = pltpu.make_async_copy(r_hbm, big_a, load.at[0])
    load_c = pltpu.make_async_copy(
        c_hbm.at[pl.ds(place.pb * 16, 16), :], c_buf, load.at[1]
    )
    load_q = pltpu.make_async_copy(q_hbm, big_b.at[0:2], load.at[2])
    load_t = pltpu.make_async_copy(t_hbm, t_buf, load.at[3])
    load_c.start()
    load_r.start()
    load_q.start()
    load_t.start()

    barrier = pltpu.get_barrier_semaphore()
    for axis in range(3):
        for step in range(1, RING):
            _, device = place.peer(axis, step)
            pl.semaphore_signal(barrier, inc=1, device_id=device, device_id_type=MESH)
    pl.semaphore_signal(
        barrier, inc=1, device_id=place.partner(), device_id_type=MESH
    )

    load_r.wait()
    for x in range(RING):

        def split_rotation(item, _):
            value = big_a[x, item // RING, item % RING].reshape(16, -1)
            high, low = split(value)
            rows = pl.ds(pl.multiple_of(256 * x + 16 * item, 16), 16)
            m_hi[rows, :] = high
            m_lo[rows, :] = low
            return 0

        lax.fori_loop(0, RING * RING, split_rotation, 0)

    load_c.wait()
    c_high, c_low = split(c_buf[...])
    c_both = jnp.concatenate([c_high, c_low], axis=0)
    for tile in range(4):
        cols = slice(256 * tile, 256 * tile + 256)
        both = dot(c_both, m_hi[:, cols], NN)
        code = jnp.tanh(both[:16] + both[16:] + dot(c_high, m_lo[:, cols], NN))
        d_c[:, cols] = 1.0 - code * code
        codes[mx, my, mz, core, :, cols] = code.astype(BF16)

    pl.semaphore_wait(barrier, 10)
    gather = Gather(place, codes, ag_send, ag_recv, agp_send, agp_recv)
    gather.start(0)

    load_q.wait()

    def query_code(block):
        def split_queries(item, _):
            at = block * 16 + item
            value = big_b[at // 32, (at // 8) % 4, (at // 2) % 4, at % 2]
            high, low = split(value)
            rows = pl.ds(pl.multiple_of(16 * at, 16), 16)
            q_hi[rows, :] = high
            q_lo[rows, :] = low
            return 0

        lax.fori_loop(0, 16, split_queries, 0)
        rows = slice(256 * block, 256 * block + 256)

        def tile_code(tile, _):
            cols = pl.ds(pl.multiple_of(256 * tile, 256), 256)
            high = q_hi[rows, :]
            value = (
                dot(high, m_hi[:, cols], NN)
                + dot(high, m_lo[:, cols], NN)
                + dot(q_lo[rows, :], m_hi[:, cols], NN)
            )
            code = jnp.tanh(value)
            d_q[rows, cols] = factor * (1.0 - code * code)
            q_bits[rows, cols] = code.astype(BF16)
            return 0

        lax.fori_loop(0, 4, tile_code, 0)

    query_code(0)
    gather.wait(0)
    gather.start(1)
    query_code(1)
    gather.wait(1)
    gather.start(2)
    for colour in range(COLOURS):
        gather.pair(colour, 0).start()
    query_code(2)
    query_code(3)

    shift_s[...] = jnp.broadcast_to(shift_s_ref[...], (128, 1024)).T
    shift_t[...] = jnp.broadcast_to(shift_t_ref[...], (128, 1024)).T
    load_t.wait()
    gather.finish()

    def weigh(item, _):
        block, half = item // 2, item % 2
        cols = pl.ds(pl.multiple_of(256 * block, 256), 256)
        rows = pl.ds(pl.multiple_of(512 * half, 512), 512)
        part = codes[block // 2, pl.ds(2 * (block % 2), 2)].reshape(256, -1)
        score = factor * dot(q_bits[rows, :], part, NT)
        down_s, down_t = shift_s[rows, :], shift_t[rows, :]
        student = jnp.exp(score - jnp.concatenate([down_s, down_s], axis=1))
        target = jnp.exp(
            t_buf[rows, cols].astype(F32) - jnp.concatenate([down_t, down_t], axis=1)
        )
        lane = lax.broadcasted_iota(jnp.int32, (1, 256), 1)
        limit = jnp.zeros((1, 256), jnp.int32)
        for slot in range(4):
            limit = jnp.where(lane // 64 == slot, counts[4 * block + slot], limit)
        live = jnp.where(lane % 64 < limit, 1.0 / live_total, 0.0)
        weights[rows, cols] = (live * (student - target)).astype(BF16)
        return 0

    lax.fori_loop(0, 16, weigh, 0)

    def pair_c(x):
        return remote(
            big_b.at[x, :, :, 1 - core],
            total_c.at[x],
            cp_send.at[x],
            cp_recv.at[x],
            place.partner(),
        )

    for x in range(RING):

        def corpus_grad(item, _):
            half, tile = item // 4, item % 4
            cols = pl.ds(pl.multiple_of(256 * tile, 256), 256)
            slots = pl.ds(pl.multiple_of(512 * x + 256 * half, 256), 256)
            part = dot(weights[:, slots], q_bits[:, cols], TN)
            big_b[x, pl.ds(2 * half, 2), :, :, :, cols] = part.reshape(2, 4, 2, 16, 256)
            return 0

        lax.fori_loop(0, 8, corpus_grad, 0)
        pair_c(x).start()

    def own_c(x):
        def add(item, _):
            at = (x, item // RING, item % RING)
            total_c[at] = total_c[at] + big_b[(*at, core)]
            return 0

        lax.fori_loop(0, RING * RING, add, 0)

    for x in range(RING):
        pair_c(x).wait()
        own_c(x)
    scatter_c = Scatter(place, total_c, lands_c, c_send, c_recv)
    scatter_c.start(0)

    def query_grad(item, _):
        half, tile = item // 4, item % 4
        cols = pl.ds(pl.multiple_of(256 * tile, 256), 256)
        rows = pl.ds(pl.multiple_of(512 * half, 512), 512)
        part = codes[:, :, :, :, :, cols].reshape(2048, 256)
        grad = d_q[rows, cols] * dot(weights[rows, :], part, NN)
        high, low = split(grad)
        m_hi[rows, cols] = high
        m_lo[rows, cols] = low
        return 0

    lax.fori_loop(0, 8, query_grad, 0)

    def rotation_grad(group):
        z_low, half = group // 2, group % 2
        acols = slice(256 * group, 256 * group + 256)

        def tile_grad(tile, _):
            cols = pl.ds(pl.multiple_of(256 * tile, 256), 256)
            high = q_hi[:, acols]
            value = (
                dot(high, m_hi[:, cols], TN)
                + dot(high, m_lo[:, cols], TN)
                + dot(q_lo[:, acols], m_hi[:, cols], TN)
            )
            for item in range(32):
                big_a[item // 8, (item // 2) % 4, 2 * (item % 2) + z_low, half, :, cols] = (
                    value[8 * item : 8 * item + 8]
                )
            return 0

        lax.fori_loop(0, 4, tile_grad, 0)

    rotation_grad(0)
    scatter_c.wait(0)
    scatter_c.start(1)
    rotation_grad(1)
    scatter_c.wait(1)
    scatter_c.start(2)
    rotation_grad(2)
    rotation_grad(3)
    scatter_c.wait(2)

    g_high, g_low = split(factor * d_c[...] * total_c[mx, my, mz])
    left = jnp.concatenate([c_high, c_high, c_low], axis=0)
    right = jnp.concatenate([g_high, g_low, g_high], axis=0)
    for group in range(4):
        z_low, half = group // 2, group % 2
        value = dot(left[:, 256 * group : 256 * group + 256], right, TN)
        for item in range(32):
            at = (item // 8, (item // 2) % 4, 2 * (item % 2) + z_low, half)
            big_a[at] = big_a[at] + value[8 * item : 8 * item + 8]

    def pair_g(x):
        return remote(
            big_a.at[x, :, :, 1 - core],
            total_g.at[x],
            gp_send.at[x],
            gp_recv.at[x],
            place.partner(),
        )

    for x in range(RING):
        pair_g(x).start()
    for x in range(RING):
        pair_g(x).wait()

        def add(item, _):
            at = (x, item // RING, item % RING)
            total_g[at] = total_g[at] + big_a[(*at, core)]
            return 0

        lax.fori_loop(0, RING * RING, add, 0)
    scatter_g = Scatter(place, total_g, lands_g, g_send, g_recv)
    for stage in range(3):
        scatter_g.start(stage)
        scatter_g.wait(stage)
    out_ref[...] = total_g[mx, my, mz]


def per_device(queries, corpus, rotation, counts, teacher, shift_student, shift_teacher):
    rows, width = queries.shape
    slots = teacher.shape[1]
    factor = 2.5 / math.sqrt(width)

    def lands(depth, dtype):
        return [
            pltpu.VMEM((RING - 1, *(RING,) * (2 - stage), depth, COLUMNS[colour][1]), dtype)
            for stage in range(3)
            for colour in range(COLOURS)
        ]

    dma = pltpu.SemaphoreType.DMA
    any_space = pl.BlockSpec(memory_space=pl.ANY)
    vmem = pl.BlockSpec(memory_space=pltpu.VMEM)
    smem = pl.BlockSpec(memory_space=pltpu.SMEM)
    return pl.pallas_call(
        functools.partial(kernel, factor, slots // 2),
        out_shape=jax.ShapeDtypeStruct((8, width), F32),
        in_specs=[any_space, any_space, any_space, smem, any_space, vmem, vmem],
        out_specs=vmem,
        scratch_shapes=[
            pltpu.VMEM((4, 4, 4, 2, 8, width), F32),
            pltpu.VMEM((4, 4, 4, 2, 16, width), F32),
            pltpu.VMEM((rows, slots), BF16),
            pltpu.VMEM((16, width), F32),
            pltpu.VMEM((width, width), BF16),
            pltpu.VMEM((width, width), BF16),
            pltpu.VMEM((rows, width), BF16),
            pltpu.VMEM((rows, width), BF16),
            pltpu.VMEM((rows, width), BF16),
            pltpu.VMEM((rows, width), F32),
            pltpu.VMEM((16, width), F32),
            pltpu.VMEM((4, 4, 4, 2, 16, width), BF16),
            pltpu.VMEM((rows, slots), BF16),
            pltpu.VMEM((rows, 128), F32),
            pltpu.VMEM((rows, 128), F32),
            pltpu.VMEM((4, 4, 4, 16, width), F32),
            pltpu.VMEM((4, 4, 4, 8, width), F32),
            *lands(16, F32),
            *lands(8, F32),
            dma((4,)),
            dma((27,)),
            dma((27,)),
            dma((12,)),
            dma((12,)),
            dma((27,)),
            dma((27,)),
            dma((4,)),
            dma((4,)),
            dma((27,)),
            dma((27,)),
            dma((4,)),
            dma((4,)),
        ],
        compiler_params=pltpu.CompilerParams(
            collective_id=0, has_side_effects=True, vmem_limit_bytes=67043328
        ),
    )(
        queries.reshape(2, 4, 4, 2, 16, width),
        corpus,
        rotation.reshape(4, 4, 4, 2, 8, width),
        counts,
        teacher,
        shift_student.reshape(1, rows),
        shift_teacher.reshape(1, rows),
    )


def solution(mesh):
    in_specs = (
        P(("pb", "col"), None),
        P("col", None),
        P(),
        P(),
        P(("pb", "col"), None),
        P(("pb", "col")),
        P(("pb", "col")),
    )
    return jax.shard_map(
        per_device,
        mesh=mesh,
        in_specs=in_specs,
        out_specs=P(("pb", "col"), None),
        check_vma=False,
    )
```

```python
import functools
import math

import jax
import jax.numpy as jnp
from jax import lax
from jax.experimental import pallas as pl
from jax.experimental.pallas import tpu as pltpu
from jax.sharding import PartitionSpec as P

MESH = pl.DeviceIdType.MESH
F32 = jnp.float32
BF16 = jnp.bfloat16

RING = 4
ORDERS = ((0, 1, 2), (1, 2, 0), (2, 0, 1))
COLUMNS = ((0, 384), (384, 384), (768, 256))
COLOURS = len(ORDERS)

LOW, HIGH = slice(0, RING // 2), slice(RING // 2, RING)
PIECES = 6


def split(value):
    high = value.astype(BF16)
    return high, (value - high.astype(F32)).astype(BF16)


def dot(a, b, dims):
    return lax.dot_general(a, b, (dims, ((), ())), preferred_element_type=F32)


NN = ((1,), (0,))
NT = ((1,), (1,))
TN = ((0,), (0,))


class Place:
    def __init__(self):
        pb, col = lax.axis_index("pb"), lax.axis_index("col")
        self.at = (col // 8, (col // 2) % 4, (col % 2) * 2 + pb // 2)
        self.core = pb % 2
        self.pb = pb

    def device(self, at, core):
        x, y, z = at
        return ((z % 2) * 2 + core, x * 8 + y * 2 + z // 2)

    def peer(self, axis, step):
        at = list(self.at)
        at[axis] = (at[axis] + step) % RING
        return at[axis], self.device(at, self.core)

    def partner(self):
        return self.device(self.at, 1 - self.core)


def remote(src, dst, send, recv, device):
    return pltpu.make_async_remote_copy(
        src_ref=src,
        dst_ref=dst,
        send_sem=send,
        recv_sem=recv,
        device_id=device,
        device_id_type=MESH,
    )


class Gather:
    def __init__(self, place, codes, send, recv, pair_send, pair_recv):
        self.place, self.codes = place, codes
        self.send, self.recv = send, recv
        self.pair_send, self.pair_recv = pair_send, pair_recv

    def region(self, colour, known, last=None, half=slice(None)):
        order, (start, width) = ORDERS[colour], COLUMNS[colour]
        index = list(self.place.at)
        for axis in order[:known]:
            index[axis] = slice(None)
        if known == 2:
            index[min(order[:2])] = half
        if last is not None:
            index[order[2]] = last
        return self.codes.at[
            index[0], index[1], index[2], self.place.core, :, start : start + width
        ]

    def copies(self, stage):
        for colour in range(COLOURS):
            part = self.region(colour, stage)
            for step in range(1, RING):
                slot = (colour * 3 + stage) * PIECES + step - 1
                _, device = self.place.peer(ORDERS[colour][stage], step)
                yield remote(
                    part, part, self.send.at[slot], self.recv.at[slot], device
                )

    def start(self, stage):
        for copy in self.copies(stage):
            copy.start()

    def wait(self, stage):
        for copy in self.copies(stage):
            copy.wait()

    def pair(self, colour, step):
        source, _ = self.place.peer(ORDERS[colour][2], -step)
        part = self.region(colour, 2, source)
        slot = colour * RING + step
        return remote(
            part,
            part,
            self.pair_send.at[slot],
            self.pair_recv.at[slot],
            self.place.partner(),
        )

    def ring(self, colour, piece):
        axis = ORDERS[colour][2]
        up = piece in (0, 1, 4)
        far, device = self.place.peer(axis, 1 if up else -1)
        source = self.place.at[axis]
        if piece > 3:
            source, _ = self.place.peer(axis, -1 if up else 1)
        half = (LOW, HIGH, HIGH, LOW, LOW, HIGH)[piece]
        part = self.region(colour, 2, source, half)
        slot = (colour * 3 + 2) * PIECES + piece
        return remote(part, part, self.send.at[slot], self.recv.at[slot], device)

    def start_ring(self):
        for piece in (0, 2, 1, 3):
            for colour in range(COLOURS):
                self.ring(colour, piece).start()

    def relay(self):
        for piece in (0, 2):
            for colour in range(COLOURS):
                self.ring(colour, piece).wait()
                self.ring(colour, 4 + piece // 2).start()

    def finish(self):
        for piece, step in ((1, 1), (3, 3)):
            for colour in range(COLOURS):
                self.ring(colour, piece).wait()
                self.pair(colour, step).start()
        for colour in range(COLOURS):
            self.ring(colour, 4).wait()
            self.ring(colour, 5).wait()
            self.pair(colour, 2).start()
        for colour in range(COLOURS):
            for step in range(RING):
                self.pair(colour, step).wait()


class Scatter:
    def __init__(self, place, total, lands, send, recv):
        self.place, self.total, self.lands = place, total, lands
        self.send, self.recv = send, recv

    def block(self, colour, at):
        (start, width) = COLUMNS[colour]
        index = [slice(None)] * 3
        index[ORDERS[colour][0]] = at
        return self.total.at[index[0], index[1], index[2], :, start : start + width]

    def ring(self, colour, piece):
        axis = ORDERS[colour][0]
        up = piece % 2 == 0
        at, device = self.place.peer(axis, 1 if up else -1)
        if piece < 2:
            at, _ = self.place.peer(axis, 2)
        half = (LOW, HIGH, HIGH, LOW, LOW, HIGH)[piece]
        land = self.lands[0][colour].at[2 if piece < 2 else piece % 2]
        slot = colour * 3 * PIECES + piece
        return remote(
            self.block(colour, at).at[half],
            land.at[half],
            self.send.at[slot],
            self.recv.at[slot],
            device,
        )

    def start_ring(self):
        for piece in range(4):
            for colour in range(COLOURS):
                self.ring(colour, piece).start()

    def relay(self):
        for piece in range(2):
            for colour in range(COLOURS):
                axis = ORDERS[colour][0]
                self.ring(colour, piece).wait()
                at, _ = self.place.peer(axis, 1 if piece == 0 else -1)
                block, land = self.block(colour, at), self.lands[0][colour]

                def add(item, _):
                    inner = (piece * 2 + item // RING, item % RING)
                    block[inner] = block[inner] + land[(2, *inner)]
                    return 0

                lax.fori_loop(0, 2 * RING, add, 0)
                self.ring(colour, 4 + piece).start()

    def finish_ring(self):
        for colour in range(COLOURS):
            for piece in range(2, PIECES):
                self.ring(colour, piece).wait()
            block, land = self.block(colour, self.place.at[ORDERS[colour][0]]), self.lands[0][colour]

            def add(item, _):
                inner = (item // RING, item % RING)
                block[inner] = block[inner] + land[(0, *inner)] + land[(1, *inner)]
                return 0

            lax.fori_loop(0, RING * RING, add, 0)

    def copies(self, stage):
        for colour in range(COLOURS):
            order, (start, width) = ORDERS[colour], COLUMNS[colour]
            for step in range(1, RING):
                slot = (colour * 3 + stage) * PIECES + step - 1
                index = [slice(None)] * 3
                for axis in order[:stage]:
                    index[axis] = self.place.at[axis]
                index[order[stage]], device = self.place.peer(order[stage], step)
                yield remote(
                    self.total.at[index[0], index[1], index[2], :, start : start + width],
                    self.lands[stage][colour].at[step - 1],
                    self.send.at[slot],
                    self.recv.at[slot],
                    device,
                )

    def start(self, stage):
        for copy in self.copies(stage):
            copy.start()

    def wait(self, stage):
        for copy in self.copies(stage):
            copy.wait()
        for colour in range(COLOURS):
            order, (start, width) = ORDERS[colour], COLUMNS[colour]
            land = self.lands[stage][colour]
            rest = sorted(order[stage + 1 :])

            def add(item, _):
                index = list(self.place.at)
                inner = [item // RING, item % RING][2 - len(rest) :]
                for axis, at in zip(rest, inner):
                    index[axis] = at
                value = self.total[
                    index[0], index[1], index[2], :, start : start + width
                ]
                for step in range(RING - 1):
                    value = value + land[(step, *inner)]
                self.total[index[0], index[1], index[2], :, start : start + width] = value
                return 0

            lax.fori_loop(0, RING ** len(rest), add, 0)


def kernel(
    factor,
    live_total,
    q_hbm,
    c_hbm,
    r_hbm,
    counts,
    t_hbm,
    shift_s_ref,
    shift_t_ref,
    out_ref,
    big_a,
    big_b,
    t_buf,
    c_buf,
    m_hi,
    m_lo,
    q_hi,
    q_lo,
    q_bits,
    d_q,
    d_c,
    codes,
    weights,
    shift_s,
    shift_t,
    total_c,
    total_g,
    turned,
    *rest,
):
    lands_c, rest = (rest[0:3], rest[3:6], rest[6:9]), rest[9:]
    lands_g, rest = (rest[0:3], rest[3:6], rest[6:9]), rest[9:]
    (
        load,
        ag_send,
        ag_recv,
        agp_send,
        agp_recv,
        c_send,
        c_recv,
        cp_send,
        cp_recv,
        g_send,
        g_recv,
        gp_send,
        gp_recv,
    ) = rest

    place = Place()
    core = place.core
    mx, my, mz = place.at

    load_r = pltpu.make_async_copy(r_hbm, big_a, load.at[0])
    load_c = pltpu.make_async_copy(
        c_hbm.at[pl.ds(place.pb * 16, 16), :], c_buf, load.at[1]
    )
    load_q = pltpu.make_async_copy(q_hbm, big_b.at[0:2], load.at[2])
    load_t = pltpu.make_async_copy(t_hbm, t_buf, load.at[3])
    load_c.start()
    load_r.start()
    load_q.start()
    load_t.start()

    barrier = pltpu.get_barrier_semaphore()
    for axis in range(3):
        for step in range(1, RING):
            _, device = place.peer(axis, step)
            pl.semaphore_signal(barrier, inc=1, device_id=device, device_id_type=MESH)
    pl.semaphore_signal(
        barrier, inc=1, device_id=place.partner(), device_id_type=MESH
    )

    load_r.wait()
    for x in range(RING):

        def split_rotation(item, _):
            value = big_a[x, item // RING, item % RING].reshape(16, -1)
            high, low = split(value)
            rows = pl.ds(pl.multiple_of(256 * x + 16 * item, 16), 16)
            m_hi[rows, :] = high
            m_lo[rows, :] = low
            return 0

        lax.fori_loop(0, RING * RING, split_rotation, 0)

    load_c.wait()
    c_high, c_low = split(c_buf[...])
    c_both = jnp.concatenate([c_high, c_low], axis=0)
    for tile in range(4):
        cols = slice(256 * tile, 256 * tile + 256)
        both = dot(c_both, m_hi[:, cols], NN)
        code = jnp.tanh(both[:16] + both[16:] + dot(c_high, m_lo[:, cols], NN))
        d_c[:, cols] = 1.0 - code * code
        codes[mx, my, mz, core, :, cols] = code.astype(BF16)

    pl.semaphore_wait(barrier, 10)
    gather = Gather(place, codes, ag_send, ag_recv, agp_send, agp_recv)
    gather.start(0)

    load_q.wait()

    def query_code(block):
        def split_queries(item, _):
            at = block * 16 + item
            value = big_b[at // 32, (at // 8) % 4, (at // 2) % 4, at % 2]
            high, low = split(value)
            rows = pl.ds(pl.multiple_of(16 * at, 16), 16)
            q_hi[rows, :] = high
            q_lo[rows, :] = low
            return 0

        lax.fori_loop(0, 16, split_queries, 0)
        rows = slice(256 * block, 256 * block + 256)

        def tile_code(tile, _):
            cols = pl.ds(pl.multiple_of(256 * tile, 256), 256)
            high = q_hi[rows, :]
            value = (
                dot(high, m_hi[:, cols], NN)
                + dot(high, m_lo[:, cols], NN)
                + dot(q_lo[rows, :], m_hi[:, cols], NN)
            )
            code = jnp.tanh(value)
            d_q[rows, cols] = factor * (1.0 - code * code)
            q_bits[rows, cols] = code.astype(BF16)
            return 0

        lax.fori_loop(0, 4, tile_code, 0)

    query_code(0)
    gather.wait(0)
    gather.start(1)
    query_code(1)
    gather.wait(1)
    gather.start_ring()
    for colour in range(COLOURS):
        gather.pair(colour, 0).start()
    query_code(2)
    gather.relay()
    query_code(3)

    shift_s[...] = jnp.broadcast_to(shift_s_ref[...], (128, 1024)).T
    shift_t[...] = jnp.broadcast_to(shift_t_ref[...], (128, 1024)).T
    load_t.wait()
    gather.finish()

    def weigh(item, _):
        block, half = item // 2, item % 2
        cols = pl.ds(pl.multiple_of(256 * block, 256), 256)
        rows = pl.ds(pl.multiple_of(512 * half, 512), 512)
        part = codes[block // 2, pl.ds(2 * (block % 2), 2)].reshape(256, -1)
        score = factor * dot(q_bits[rows, :], part, NT)
        down_s, down_t = shift_s[rows, :], shift_t[rows, :]
        student = jnp.exp(score - jnp.concatenate([down_s, down_s], axis=1))
        target = jnp.exp(
            t_buf[rows, cols].astype(F32) - jnp.concatenate([down_t, down_t], axis=1)
        )
        lane = lax.broadcasted_iota(jnp.int32, (1, 256), 1)
        limit = jnp.zeros((1, 256), jnp.int32)
        for slot in range(4):
            limit = jnp.where(lane // 64 == slot, counts[4 * block + slot], limit)
        live = jnp.where(lane % 64 < limit, 1.0 / live_total, 0.0)
        weights[rows, cols] = (live * (student - target)).astype(BF16)
        return 0

    lax.fori_loop(0, 16, weigh, 0)

    def pair_c(x):
        return remote(
            big_b.at[x, :, :, 1 - core],
            total_c.at[x],
            cp_send.at[x],
            cp_recv.at[x],
            place.partner(),
        )

    for group in range(8):
        turned[0:256, :] = weights[:, 256 * group : 256 * group + 256].T

        def corpus_grad(tile, _):
            cols = pl.ds(pl.multiple_of(256 * tile, 256), 256)
            part = dot(turned[0:256, :], q_bits[:, cols], NN)
            half = slice(2 * (group % 2), 2 * (group % 2) + 2)
            big_b[group // 2, half, :, :, :, cols] = part.reshape(2, 4, 2, 16, 256)
            return 0

        lax.fori_loop(0, 4, corpus_grad, 0)
        if group % 2:
            pair_c(group // 2).start()

    def own_c(x):
        def add(item, _):
            at = (x, item // RING, item % RING)
            total_c[at] = total_c[at] + big_b[(*at, core)]
            return 0

        lax.fori_loop(0, RING * RING, add, 0)

    for x in range(RING):
        pair_c(x).wait()
        own_c(x)
    scatter_c = Scatter(place, total_c, lands_c, c_send, c_recv)
    scatter_c.start_ring()

    def query_grad(item, _):
        half, tile = item // 4, item % 4
        cols = pl.ds(pl.multiple_of(256 * tile, 256), 256)
        rows = pl.ds(pl.multiple_of(512 * half, 512), 512)
        part = codes[:, :, :, :, :, cols].reshape(2048, 256)
        grad = d_q[rows, cols] * dot(weights[rows, :], part, NN)
        high, low = split(grad)
        m_hi[rows, cols] = high
        m_lo[rows, cols] = low
        return 0

    lax.fori_loop(0, 8, query_grad, 0)

    def rotation_grad(group):
        z_low, half = group // 2, group % 2
        acols = slice(256 * group, 256 * group + 256)
        turned[0:256, :] = q_hi[:, acols].T
        turned[256:512, :] = q_lo[:, acols].T

        def tile_grad(tile, _):
            cols = pl.ds(pl.multiple_of(256 * tile, 256), 256)
            both = dot(turned[...], m_hi[:, cols], NN)
            value = both[:256] + both[256:] + dot(turned[0:256, :], m_lo[:, cols], NN)
            for item in range(32):
                big_a[item // 8, (item // 2) % 4, 2 * (item % 2) + z_low, half, :, cols] = (
                    value[8 * item : 8 * item + 8]
                )
            return 0

        lax.fori_loop(0, 4, tile_grad, 0)

    scatter_c.relay()
    rotation_grad(0)
    rotation_grad(1)
    rotation_grad(2)
    scatter_c.finish_ring()
    scatter_c.start(1)
    rotation_grad(3)
    scatter_c.wait(1)
    scatter_c.start(2)
    scatter_c.wait(2)

    g_high, g_low = split(factor * d_c[...] * total_c[mx, my, mz])
    left = jnp.concatenate([c_high, c_high, c_low], axis=0)
    right = jnp.concatenate([g_high, g_low, g_high], axis=0)
    for group in range(4):
        z_low, half = group // 2, group % 2
        value = dot(left[:, 256 * group : 256 * group + 256], right, TN)
        for item in range(32):
            at = (item // 8, (item // 2) % 4, 2 * (item % 2) + z_low, half)
            big_a[at] = big_a[at] + value[8 * item : 8 * item + 8]

    def pair_g(x):
        return remote(
            big_a.at[x, :, :, 1 - core],
            total_g.at[x],
            gp_send.at[x],
            gp_recv.at[x],
            place.partner(),
        )

    for x in range(RING):
        pair_g(x).start()
    for x in range(RING):
        pair_g(x).wait()

        def add(item, _):
            at = (x, item // RING, item % RING)
            total_g[at] = total_g[at] + big_a[(*at, core)]
            return 0

        lax.fori_loop(0, RING * RING, add, 0)
    scatter_g = Scatter(place, total_g, lands_g, g_send, g_recv)
    scatter_g.start_ring()
    scatter_g.relay()
    scatter_g.finish_ring()
    for stage in (1, 2):
        scatter_g.start(stage)
        scatter_g.wait(stage)
    out_ref[...] = total_g[mx, my, mz]


def per_device(queries, corpus, rotation, counts, teacher, shift_student, shift_teacher):
    rows, width = queries.shape
    slots = teacher.shape[1]
    factor = 2.5 / math.sqrt(width)

    def lands(depth, dtype):
        return [
            pltpu.VMEM((RING - 1, *(RING,) * (2 - stage), depth, COLUMNS[colour][1]), dtype)
            for stage in range(3)
            for colour in range(COLOURS)
        ]

    dma = pltpu.SemaphoreType.DMA
    any_space = pl.BlockSpec(memory_space=pl.ANY)
    vmem = pl.BlockSpec(memory_space=pltpu.VMEM)
    smem = pl.BlockSpec(memory_space=pltpu.SMEM)
    return pl.pallas_call(
        functools.partial(kernel, factor, slots // 2),
        out_shape=jax.ShapeDtypeStruct((8, width), F32),
        in_specs=[any_space, any_space, any_space, smem, any_space, vmem, vmem],
        out_specs=vmem,
        scratch_shapes=[
            pltpu.VMEM((4, 4, 4, 2, 8, width), F32),
            pltpu.VMEM((4, 4, 4, 2, 16, width), F32),
            pltpu.VMEM((rows, slots), BF16),
            pltpu.VMEM((16, width), F32),
            pltpu.VMEM((width, width), BF16),
            pltpu.VMEM((width, width), BF16),
            pltpu.VMEM((rows, width), BF16),
            pltpu.VMEM((rows, width), BF16),
            pltpu.VMEM((rows, width), BF16),
            pltpu.VMEM((rows, width), F32),
            pltpu.VMEM((16, width), F32),
            pltpu.VMEM((4, 4, 4, 2, 16, width), BF16),
            pltpu.VMEM((rows, slots), BF16),
            pltpu.VMEM((rows, 128), F32),
            pltpu.VMEM((rows, 128), F32),
            pltpu.VMEM((4, 4, 4, 16, width), F32),
            pltpu.VMEM((4, 4, 4, 8, width), F32),
            pltpu.VMEM((512, rows), BF16),
            *lands(16, F32),
            *lands(8, F32),
            dma((4,)),
            dma((54,)),
            dma((54,)),
            dma((12,)),
            dma((12,)),
            dma((54,)),
            dma((54,)),
            dma((4,)),
            dma((4,)),
            dma((54,)),
            dma((54,)),
            dma((4,)),
            dma((4,)),
        ],
        compiler_params=pltpu.CompilerParams(
            collective_id=0, has_side_effects=True, vmem_limit_bytes=67043328
        ),
    )(
        queries.reshape(2, 4, 4, 2, 16, width),
        corpus,
        rotation.reshape(4, 4, 4, 2, 8, width),
        counts,
        teacher,
        shift_student.reshape(1, rows),
        shift_teacher.reshape(1, rows),
    )


def solution(mesh):
    in_specs = (
        P(("pb", "col"), None),
        P("col", None),
        P(),
        P(),
        P(("pb", "col"), None),
        P(("pb", "col")),
        P(("pb", "col")),
    )
    return jax.shard_map(
        per_device,
        mesh=mesh,
        in_specs=in_specs,
        out_specs=P(("pb", "col"), None),
        check_vma=False,
    )
```

```python
import functools
import math

import jax
import jax.numpy as jnp
from jax import lax
from jax.experimental import pallas as pl
from jax.experimental.pallas import tpu as pltpu
from jax.sharding import PartitionSpec as P

MESH = pl.DeviceIdType.MESH
F32 = jnp.float32
BF16 = jnp.bfloat16

RING = 4
ORDERS = ((0, 1, 2), (1, 2, 0), (2, 0, 1))
COLUMNS = ((0, 384), (384, 384), (768, 256))
COLOURS = len(ORDERS)

LOW, HIGH = slice(0, RING // 2), slice(RING // 2, RING)
PIECES = 6


def split(value):
    high = value.astype(BF16)
    return high, (value - high.astype(F32)).astype(BF16)


def dot(a, b, dims):
    return lax.dot_general(a, b, (dims, ((), ())), preferred_element_type=F32)


NN = ((1,), (0,))
NT = ((1,), (1,))
TN = ((0,), (0,))


class Place:
    def __init__(self):
        pb, col = lax.axis_index("pb"), lax.axis_index("col")
        self.at = (col // 8, (col // 2) % 4, (col % 2) * 2 + pb // 2)
        self.core = pb % 2
        self.pb = pb

    def device(self, at, core):
        x, y, z = at
        return ((z % 2) * 2 + core, x * 8 + y * 2 + z // 2)

    def peer(self, axis, step):
        at = list(self.at)
        at[axis] = (at[axis] + step) % RING
        return at[axis], self.device(at, self.core)

    def partner(self):
        return self.device(self.at, 1 - self.core)


def remote(src, dst, send, recv, device):
    return pltpu.make_async_remote_copy(
        src_ref=src,
        dst_ref=dst,
        send_sem=send,
        recv_sem=recv,
        device_id=device,
        device_id_type=MESH,
    )


class Gather:
    def __init__(self, place, codes, send, recv, pair_send, pair_recv):
        self.place, self.codes = place, codes
        self.send, self.recv = send, recv
        self.pair_send, self.pair_recv = pair_send, pair_recv

    def region(self, colour, known, last=None, half=slice(None)):
        order, (start, width) = ORDERS[colour], COLUMNS[colour]
        index = list(self.place.at)
        for axis in order[:known]:
            index[axis] = slice(None)
        if known == 2:
            index[min(order[:2])] = half
        if last is not None:
            index[order[2]] = last
        return self.codes.at[
            index[0], index[1], index[2], self.place.core, :, start : start + width
        ]

    def copies(self, stage):
        for colour in range(COLOURS):
            part = self.region(colour, stage)
            for step in range(1, RING):
                slot = (colour * 3 + stage) * PIECES + step - 1
                _, device = self.place.peer(ORDERS[colour][stage], step)
                yield remote(
                    part, part, self.send.at[slot], self.recv.at[slot], device
                )

    def start(self, stage):
        for copy in self.copies(stage):
            copy.start()

    def wait(self, stage):
        for copy in self.copies(stage):
            copy.wait()

    def pair(self, colour, step):
        source, _ = self.place.peer(ORDERS[colour][2], -step)
        part = self.region(colour, 2, source)
        slot = colour * RING + step
        return remote(
            part,
            part,
            self.pair_send.at[slot],
            self.pair_recv.at[slot],
            self.place.partner(),
        )

    def ring(self, colour, piece):
        axis = ORDERS[colour][2]
        up = piece in (0, 1, 4)
        far, device = self.place.peer(axis, 1 if up else -1)
        source = self.place.at[axis]
        if piece > 3:
            source, _ = self.place.peer(axis, -1 if up else 1)
        half = (LOW, HIGH, HIGH, LOW, LOW, HIGH)[piece]
        part = self.region(colour, 2, source, half)
        slot = (colour * 3 + 2) * PIECES + piece
        return remote(part, part, self.send.at[slot], self.recv.at[slot], device)

    def start_ring(self):
        for piece in (0, 2, 1, 3):
            for colour in range(COLOURS):
                self.ring(colour, piece).start()

    def relay(self):
        for piece in (0, 2):
            for colour in range(COLOURS):
                self.ring(colour, piece).wait()
                self.ring(colour, 4 + piece // 2).start()

    def finish(self):
        for piece, step in ((1, 1), (3, 3)):
            for colour in range(COLOURS):
                self.ring(colour, piece).wait()
                self.pair(colour, step).start()
        for colour in range(COLOURS):
            self.ring(colour, 4).wait()
            self.ring(colour, 5).wait()
            self.pair(colour, 2).start()
        for colour in range(COLOURS):
            for step in range(RING):
                self.pair(colour, step).wait()


class Scatter:
    def __init__(self, place, total, sent, lands, send, recv):
        self.place, self.total, self.sent, self.lands = place, total, sent, lands
        self.send, self.recv = send, recv

    def block(self, ref, colour, at):
        start, width = COLUMNS[colour]
        index = [slice(None)] * 3
        index[ORDERS[colour][0]] = at
        return ref.at[index[0], index[1], index[2], :, start : start + width]

    def ring(self, colour, piece):
        axis = ORDERS[colour][0]
        up = piece % 2 == 0
        at, device = self.place.peer(axis, 1 if up else -1)
        if piece < 2:
            at, _ = self.place.peer(axis, 2)
        half = (LOW, HIGH, HIGH, LOW, LOW, HIGH)[piece]
        land = self.lands[0][colour].at[2 if piece < 2 else piece % 2]
        slot = colour * 3 * PIECES + piece
        return remote(
            self.block(self.sent, colour, at).at[half],
            land.at[half],
            self.send.at[slot],
            self.recv.at[slot],
            device,
        )

    def start_ring(self):
        for piece in range(4):
            for colour in range(COLOURS):
                self.ring(colour, piece).start()

    def relay(self):
        for piece in range(2):
            for colour in range(COLOURS):
                axis = ORDERS[colour][0]
                self.ring(colour, piece).wait()
                at, _ = self.place.peer(axis, 1 if piece == 0 else -1)
                block, land = self.block(self.total, colour, at), self.lands[0][colour]
                sent = self.block(self.sent, colour, at)

                def add(item, _):
                    inner = (piece * 2 + item // RING, item % RING)
                    value = block[inner] + land[(2, *inner)].astype(F32)
                    sent[inner] = value.astype(sent.dtype)
                    return 0

                lax.fori_loop(0, 2 * RING, add, 0)
                self.ring(colour, 4 + piece).start()

    def finish_ring(self):
        for colour in range(COLOURS):
            for piece in range(2, PIECES):
                self.ring(colour, piece).wait()
            at = self.place.at[ORDERS[colour][0]]
            block, land = self.block(self.total, colour, at), self.lands[0][colour]

            def add(item, _):
                inner = (item // RING, item % RING)
                first, second = land[(0, *inner)], land[(1, *inner)]
                block[inner] = block[inner] + first.astype(F32) + second.astype(F32)
                return 0

            lax.fori_loop(0, RING * RING, add, 0)

    def copies(self, stage):
        for colour in range(COLOURS):
            order, (start, width) = ORDERS[colour], COLUMNS[colour]
            for step in range(1, RING):
                slot = (colour * 3 + stage) * PIECES + step - 1
                index = [slice(None)] * 3
                for axis in order[:stage]:
                    index[axis] = self.place.at[axis]
                index[order[stage]], device = self.place.peer(order[stage], step)
                yield remote(
                    self.total.at[index[0], index[1], index[2], :, start : start + width],
                    self.lands[stage][colour].at[step - 1],
                    self.send.at[slot],
                    self.recv.at[slot],
                    device,
                )

    def start(self, stage):
        for copy in self.copies(stage):
            copy.start()

    def wait(self, stage):
        for copy in self.copies(stage):
            copy.wait()
        for colour in range(COLOURS):
            order, (start, width) = ORDERS[colour], COLUMNS[colour]
            land = self.lands[stage][colour]
            rest = sorted(order[stage + 1 :])

            def add(item, _):
                index = list(self.place.at)
                inner = [item // RING, item % RING][2 - len(rest) :]
                for axis, at in zip(rest, inner):
                    index[axis] = at
                value = self.total[
                    index[0], index[1], index[2], :, start : start + width
                ]
                for step in range(RING - 1):
                    value = value + land[(step, *inner)]
                self.total[index[0], index[1], index[2], :, start : start + width] = value
                return 0

            lax.fori_loop(0, RING ** len(rest), add, 0)


def kernel(
    factor,
    live_total,
    q_hbm,
    c_hbm,
    r_hbm,
    counts,
    t_hbm,
    shift_s_ref,
    shift_t_ref,
    out_ref,
    big_a,
    big_b,
    t_buf,
    c_buf,
    m_hi,
    m_lo,
    q_hi,
    q_lo,
    q_bits,
    d_q,
    d_c,
    codes,
    weights,
    shift_s,
    shift_t,
    total_c,
    total_g,
    turned,
    sent_c,
    slopes,
    c_left,
    c_right,
    *rest,
):
    lands_c, rest = (rest[0:3], rest[3:6], rest[6:9]), rest[9:]
    lands_g, rest = (rest[0:3], rest[3:6], rest[6:9]), rest[9:]
    (
        load,
        ag_send,
        ag_recv,
        agp_send,
        agp_recv,
        c_send,
        c_recv,
        cp_send,
        cp_recv,
        g_send,
        g_recv,
        gp_send,
        gp_recv,
        swap_send,
        swap_recv,
    ) = rest

    place = Place()
    core = place.core
    mx, my, mz = place.at

    load_r = pltpu.make_async_copy(r_hbm, big_a, load.at[0])
    load_c = pltpu.make_async_copy(
        c_hbm.at[pl.ds((place.pb // 2) * 32, 32), :], c_buf, load.at[1]
    )
    load_q = pltpu.make_async_copy(q_hbm, big_b.at[0:2], load.at[2])
    load_t = pltpu.make_async_copy(t_hbm, t_buf, load.at[3])
    load_c.start()
    load_r.start()
    load_q.start()
    load_t.start()

    barrier = pltpu.get_barrier_semaphore()
    for axis in range(3):
        for step in range(1, RING):
            _, device = place.peer(axis, step)
            pl.semaphore_signal(barrier, inc=1, device_id=device, device_id_type=MESH)
    pl.semaphore_signal(
        barrier, inc=1, device_id=place.partner(), device_id_type=MESH
    )

    load_r.wait()
    for x in range(RING):

        def split_rotation(item, _):
            value = big_a[x, item // RING, item % RING].reshape(16, -1)
            high, low = split(value)
            rows = pl.ds(pl.multiple_of(256 * x + 16 * item, 16), 16)
            m_hi[rows, :] = high
            m_lo[rows, :] = low
            return 0

        lax.fori_loop(0, RING * RING, split_rotation, 0)

    load_c.wait()
    c_high, c_low = split(c_buf[...])
    c_left[...] = jnp.concatenate([c_high, c_high, c_low], axis=0)
    c_high, c_low = split(c_buf[pl.ds(pl.multiple_of(16 * core, 16), 16), :])
    c_both = jnp.concatenate([c_high, c_low], axis=0)
    for tile in range(4):
        cols = slice(256 * tile, 256 * tile + 256)
        both = dot(c_both, m_hi[:, cols], NN)
        code = jnp.tanh(both[:16] + both[16:] + dot(c_high, m_lo[:, cols], NN))
        d_c[:, cols] = 1.0 - code * code
        codes[mx, my, mz, core, :, cols] = code.astype(BF16)

    pl.semaphore_wait(barrier, 10)
    gather = Gather(place, codes, ag_send, ag_recv, agp_send, agp_recv)
    gather.start(0)

    load_q.wait()

    def query_code(block, first):
        def split_queries(item, _):
            at = block * 32 + item
            value = big_b[at // 32, (at // 8) % 4, (at // 2) % 4, at % 2]
            high, low = split(value)
            rows = pl.ds(pl.multiple_of(16 * at, 16), 16)
            q_hi[rows, :] = high
            q_lo[rows, :] = low
            return 0

        if first == 0:
            lax.fori_loop(0, 32, split_queries, 0)
        rows = slice(512 * block, 512 * block + 512)

        def tile_code(tile, _):
            cols = pl.ds(pl.multiple_of(256 * tile, 256), 256)
            high = q_hi[rows, :]
            value = (
                dot(high, m_hi[:, cols], NN)
                + dot(q_lo[rows, :], m_hi[:, cols], NN)
                + dot(high, m_lo[:, cols], NN)
            )
            code = jnp.tanh(value)
            d_q[rows, cols] = factor * (1.0 - code * code)
            q_bits[rows, cols] = code.astype(BF16)
            return 0

        lax.fori_loop(first, first + 2, tile_code, 0)

    query_code(0, 0)
    gather.wait(0)
    gather.start(1)
    query_code(0, 2)
    gather.wait(1)
    gather.start_ring()
    for colour in range(COLOURS):
        gather.pair(colour, 0).start()
    query_code(1, 0)
    gather.relay()
    query_code(1, 2)

    shift_s[...] = jnp.broadcast_to(shift_s_ref[...], (128, 1024)).T
    shift_t[...] = jnp.broadcast_to(shift_t_ref[...], (128, 1024)).T
    load_t.wait()
    gather.finish()

    def weigh(item, _):
        block, half = item // 2, item % 2
        cols = pl.ds(pl.multiple_of(256 * block, 256), 256)
        rows = pl.ds(pl.multiple_of(512 * half, 512), 512)
        part = codes[block // 2, pl.ds(2 * (block % 2), 2)].reshape(256, -1)
        score = factor * dot(q_bits[rows, :], part, NT)
        down_s, down_t = shift_s[rows, :], shift_t[rows, :]
        student = jnp.exp(score - jnp.concatenate([down_s, down_s], axis=1))
        target = jnp.exp(
            t_buf[rows, cols].astype(F32) - jnp.concatenate([down_t, down_t], axis=1)
        )
        lane = lax.broadcasted_iota(jnp.int32, (1, 256), 1)
        limit = jnp.zeros((1, 256), jnp.int32)
        for slot in range(4):
            limit = jnp.where(lane // 64 == slot, counts[4 * block + slot], limit)
        live = jnp.where(lane % 64 < limit, 1.0 / live_total, 0.0)
        weights[rows, cols] = (live * (student - target)).astype(BF16)
        return 0

    lax.fori_loop(0, 16, weigh, 0)

    def pair_c(x):
        return remote(
            big_b.at[x, :, :, 1 - core],
            total_c.at[x],
            cp_send.at[x],
            cp_recv.at[x],
            place.partner(),
        )

    for x in range(RING):
        turned[0:512, :] = weights[:, 512 * x : 512 * x + 512].T

        def corpus_grad(tile, _):
            cols = pl.ds(pl.multiple_of(256 * tile, 256), 256)
            part = dot(turned[0:512, :], q_bits[:, cols], NN)
            big_b[x, :, :, :, :, cols] = part.reshape(4, 4, 2, 16, 256)
            return 0

        lax.fori_loop(0, 4, corpus_grad, 0)
        pair_c(x).start()

    def own_c(x):
        def add(item, _):
            at = (x, item // RING, item % RING)
            value = total_c[at] + big_b[(*at, core)]
            total_c[at] = value
            sent_c[at] = value.astype(BF16)
            return 0

        lax.fori_loop(0, RING * RING, add, 0)

    for x in range(RING):
        pair_c(x).wait()
        own_c(x)
    scatter_c = Scatter(place, total_c, sent_c, lands_c, c_send, c_recv)
    scatter_c.start_ring()

    def query_grad(item, _):
        half, tile = item // 4, item % 4
        cols = pl.ds(pl.multiple_of(256 * tile, 256), 256)
        rows = pl.ds(pl.multiple_of(512 * half, 512), 512)
        part = codes[:, :, :, :, :, cols].reshape(2048, 256)
        grad = d_q[rows, cols] * dot(weights[rows, :], part, NN)
        high, low = split(grad)
        m_hi[rows, cols] = high
        m_lo[rows, cols] = low
        return 0

    lax.fori_loop(0, 8, query_grad, 0)

    def group_cols(z_low, half):
        return pl.ds(pl.multiple_of(256 * (2 * z_low + half), 256), 256)

    def turn(half):
        for z_low in range(2):
            rows = slice(256 * z_low, 256 * z_low + 256)
            turned[rows, :] = q_hi[:, group_cols(z_low, half)].T
            rows = slice(512 + 256 * z_low, 512 + 256 * z_low + 256)
            turned[rows, :] = q_lo[:, group_cols(z_low, half)].T

    def rotation_grad(half, first):
        def tile_grad(tile, _):
            cols = pl.ds(pl.multiple_of(256 * tile, 256), 256)
            value = (
                dot(turned[0:512, :], m_hi[:, cols], NN)
                + dot(turned[512:1024, :], m_hi[:, cols], NN)
                + dot(turned[0:512, :], m_lo[:, cols], NN)
            )
            for item in range(64):
                z = 2 * (item % 2) + item // 32
                big_a[(item // 8) % 4, (item // 2) % 4, z, half, :, cols] = value[
                    8 * item : 8 * item + 8
                ]
            return 0

        lax.fori_loop(first, first + 2, tile_grad, 0)

    def pair_g(x):
        return remote(
            big_a.at[x, :, :, 1 - core],
            total_g.at[x],
            gp_send.at[x],
            gp_recv.at[x],
            place.partner(),
        )

    scatter_c.relay()
    turn(1 - core)
    rotation_grad(1 - core, 0)
    rotation_grad(1 - core, 2)
    for x in range(RING):
        pair_g(x).start()
    turn(core)
    scatter_c.finish_ring()
    scatter_c.start(1)
    rotation_grad(core, 0)
    rotation_grad(core, 2)
    scatter_c.wait(1)
    scatter_c.start(2)
    for x in range(RING):
        pair_g(x).wait()
    scatter_c.wait(2)

    slopes[core] = factor * d_c[...] * total_c[mx, my, mz]
    swap = remote(
        slopes.at[core], slopes.at[core], swap_send.at[0], swap_recv.at[0], place.partner()
    )
    swap.start()
    swap.wait()
    g_high, g_low = split(slopes[...].reshape(32, -1))
    c_right[...] = jnp.concatenate([g_high, g_low, g_high], axis=0)

    def corpus_term(tile, _):
        cols = pl.ds(pl.multiple_of(256 * tile, 256), 256)
        for z_low in range(2):
            value = dot(c_left[:, group_cols(z_low, core)], c_right[:, cols], TN)
            for item in range(32):
                at = (item // 8, (item // 2) % 4, 2 * (item % 2) + z_low)
                total_g[(*at, slice(None), cols)] = (
                    total_g[(*at, slice(None), cols)]
                    + big_a[(*at, core, slice(None), cols)]
                    + value[8 * item : 8 * item + 8]
                )
        return 0

    lax.fori_loop(0, 4, corpus_term, 0)
    scatter_g = Scatter(place, total_g, total_g, lands_g, g_send, g_recv)
    scatter_g.start_ring()
    scatter_g.relay()
    scatter_g.finish_ring()
    for stage in (1, 2):
        scatter_g.start(stage)
        scatter_g.wait(stage)
    out_ref[...] = total_g[mx, my, mz]


def per_device(queries, corpus, rotation, counts, teacher, shift_student, shift_teacher):
    rows, width = queries.shape
    slots = teacher.shape[1]
    factor = 2.5 / math.sqrt(width)

    def lands(depth, first_dtype):
        return [
            pltpu.VMEM((RING - 1, *(RING,) * (2 - stage), depth, COLUMNS[colour][1]), (first_dtype, F32, F32)[stage])
            for stage in range(3)
            for colour in range(COLOURS)
        ]

    dma = pltpu.SemaphoreType.DMA
    any_space = pl.BlockSpec(memory_space=pl.ANY)
    vmem = pl.BlockSpec(memory_space=pltpu.VMEM)
    smem = pl.BlockSpec(memory_space=pltpu.SMEM)
    return pl.pallas_call(
        functools.partial(kernel, factor, slots // 2),
        out_shape=jax.ShapeDtypeStruct((8, width), F32),
        in_specs=[any_space, any_space, any_space, smem, any_space, vmem, vmem],
        out_specs=vmem,
        scratch_shapes=[
            pltpu.VMEM((4, 4, 4, 2, 8, width), F32),
            pltpu.VMEM((4, 4, 4, 2, 16, width), F32),
            pltpu.VMEM((rows, slots), BF16),
            pltpu.VMEM((32, width), F32),
            pltpu.VMEM((width, width), BF16),
            pltpu.VMEM((width, width), BF16),
            pltpu.VMEM((rows, width), BF16),
            pltpu.VMEM((rows, width), BF16),
            pltpu.VMEM((rows, width), BF16),
            pltpu.VMEM((rows, width), F32),
            pltpu.VMEM((16, width), F32),
            pltpu.VMEM((4, 4, 4, 2, 16, width), BF16),
            pltpu.VMEM((rows, slots), BF16),
            pltpu.VMEM((rows, 128), F32),
            pltpu.VMEM((rows, 128), F32),
            pltpu.VMEM((4, 4, 4, 16, width), F32),
            pltpu.VMEM((4, 4, 4, 8, width), F32),
            pltpu.VMEM((1024, rows), BF16),
            pltpu.VMEM((4, 4, 4, 16, width), BF16),
            pltpu.VMEM((2, 16, width), F32),
            pltpu.VMEM((96, width), BF16),
            pltpu.VMEM((96, width), BF16),
            *lands(16, BF16),
            *lands(8, F32),
            dma((4,)),
            dma((54,)),
            dma((54,)),
            dma((12,)),
            dma((12,)),
            dma((54,)),
            dma((54,)),
            dma((4,)),
            dma((4,)),
            dma((54,)),
            dma((54,)),
            dma((4,)),
            dma((4,)),
            dma((1,)),
            dma((1,)),
        ],
        compiler_params=pltpu.CompilerParams(
            collective_id=0, has_side_effects=True, vmem_limit_bytes=67043328
        ),
    )(
        queries.reshape(2, 4, 4, 2, 16, width),
        corpus,
        rotation.reshape(4, 4, 4, 2, 8, width),
        counts,
        teacher,
        shift_student.reshape(1, rows),
        shift_teacher.reshape(1, rows),
    )


def solution(mesh):
    in_specs = (
        P(("pb", "col"), None),
        P("col", None),
        P(),
        P(),
        P(("pb", "col"), None),
        P(("pb", "col")),
        P(("pb", "col")),
    )
    return jax.shard_map(
        per_device,
        mesh=mesh,
        in_specs=in_specs,
        out_specs=P(("pb", "col"), None),
        check_vma=False,
    )
```

```python
import functools
import math

import jax
import jax.numpy as jnp
from jax import lax
from jax.experimental import pallas as pl
from jax.experimental.pallas import tpu as pltpu
from jax.sharding import PartitionSpec as P

MESH = pl.DeviceIdType.MESH
F32 = jnp.float32
BF16 = jnp.bfloat16

RING = 4
ORDERS = ((0, 1, 2), (1, 2, 0), (2, 0, 1))
COLUMNS = ((0, 384), (384, 384), (768, 256))
COLOURS = len(ORDERS)

LOW, HIGH = slice(0, RING // 2), slice(RING // 2, RING)
PIECES = 6


def split(value):
    high = value.astype(BF16)
    return high, (value - high.astype(F32)).astype(BF16)


def dot(a, b, dims):
    return lax.dot_general(a, b, (dims, ((), ())), preferred_element_type=F32)


NN = ((1,), (0,))
NT = ((1,), (1,))
TN = ((0,), (0,))


class Place:
    def __init__(self):
        pb, col = lax.axis_index("pb"), lax.axis_index("col")
        self.at = (col // 8, (col // 2) % 4, (col % 2) * 2 + pb // 2)
        self.core = pb % 2
        self.pb = pb

    def device(self, at, core):
        x, y, z = at
        return ((z % 2) * 2 + core, x * 8 + y * 2 + z // 2)

    def peer(self, axis, step):
        at = list(self.at)
        at[axis] = (at[axis] + step) % RING
        return at[axis], self.device(at, self.core)

    def partner(self):
        return self.device(self.at, 1 - self.core)


def remote(src, dst, send, recv, device):
    return pltpu.make_async_remote_copy(
        src_ref=src,
        dst_ref=dst,
        send_sem=send,
        recv_sem=recv,
        device_id=device,
        device_id_type=MESH,
    )


class Gather:
    def __init__(self, place, codes, send, recv, pair_send, pair_recv):
        self.place, self.codes = place, codes
        self.send, self.recv = send, recv
        self.pair_send, self.pair_recv = pair_send, pair_recv

    def region(self, colour, known, last=None, half=slice(None)):
        order, (start, width) = ORDERS[colour], COLUMNS[colour]
        index = list(self.place.at)
        for axis in order[:known]:
            index[axis] = slice(None)
        if known == 2:
            index[min(order[:2])] = half
        if last is not None:
            index[order[2]] = last
        return self.codes.at[
            index[0], index[1], index[2], self.place.core, :, start : start + width
        ]

    def copies(self, stage):
        for colour in range(COLOURS):
            part = self.region(colour, stage)
            for step in range(1, RING):
                slot = (colour * 3 + stage) * PIECES + step - 1
                _, device = self.place.peer(ORDERS[colour][stage], step)
                yield remote(
                    part, part, self.send.at[slot], self.recv.at[slot], device
                )

    def start(self, stage):
        for copy in self.copies(stage):
            copy.start()

    def wait(self, stage):
        for copy in self.copies(stage):
            copy.wait()

    def pair(self, colour, step):
        source, _ = self.place.peer(ORDERS[colour][2], -step)
        part = self.region(colour, 2, source)
        slot = colour * RING + step
        return remote(
            part,
            part,
            self.pair_send.at[slot],
            self.pair_recv.at[slot],
            self.place.partner(),
        )

    def ring(self, colour, piece):
        axis = ORDERS[colour][2]
        up = piece in (0, 1, 4)
        far, device = self.place.peer(axis, 1 if up else -1)
        source = self.place.at[axis]
        if piece > 3:
            source, _ = self.place.peer(axis, -1 if up else 1)
        half = (LOW, HIGH, HIGH, LOW, LOW, HIGH)[piece]
        part = self.region(colour, 2, source, half)
        slot = (colour * 3 + 2) * PIECES + piece
        return remote(part, part, self.send.at[slot], self.recv.at[slot], device)

    def start_ring(self):
        for piece in (0, 2, 1, 3):
            for colour in range(COLOURS):
                self.ring(colour, piece).start()

    def relay(self):
        for piece in (0, 2):
            for colour in range(COLOURS):
                self.ring(colour, piece).wait()
                self.ring(colour, 4 + piece // 2).start()

    def finish(self):
        for piece, step in ((1, 1), (3, 3)):
            for colour in range(COLOURS):
                self.ring(colour, piece).wait()
                self.pair(colour, step).start()
        for colour in range(COLOURS):
            self.ring(colour, 4).wait()
            self.ring(colour, 5).wait()
            self.pair(colour, 2).start()
        for colour in range(COLOURS):
            for step in range(RING):
                self.pair(colour, step).wait()


class Scatter:
    def __init__(self, place, total, sent, lands, send, recv):
        self.place, self.total, self.sent, self.lands = place, total, sent, lands
        self.send, self.recv = send, recv

    def block(self, ref, colour, at):
        start, width = COLUMNS[colour]
        index = [slice(None)] * 3
        index[ORDERS[colour][0]] = at
        return ref.at[index[0], index[1], index[2], :, start : start + width]

    def ring(self, colour, piece):
        axis = ORDERS[colour][0]
        up = piece % 2 == 0
        at, device = self.place.peer(axis, 1 if up else -1)
        if piece < 2:
            at, _ = self.place.peer(axis, 2)
        half = (LOW, HIGH, HIGH, LOW, LOW, HIGH)[piece]
        land = self.lands[0][colour].at[2 if piece < 2 else piece % 2]
        slot = colour * 3 * PIECES + piece
        return remote(
            self.block(self.sent, colour, at).at[half],
            land.at[half],
            self.send.at[slot],
            self.recv.at[slot],
            device,
        )

    def start_ring(self):
        for piece in range(4):
            for colour in range(COLOURS):
                self.ring(colour, piece).start()

    def relay(self):
        for piece in range(2):
            for colour in range(COLOURS):
                axis = ORDERS[colour][0]
                self.ring(colour, piece).wait()
                at, _ = self.place.peer(axis, 1 if piece == 0 else -1)
                block, land = self.block(self.total, colour, at), self.lands[0][colour]
                sent = self.block(self.sent, colour, at)

                def add(item, _):
                    inner = (piece * 2 + item // RING, item % RING)
                    value = block[inner] + land[(2, *inner)].astype(F32)
                    sent[inner] = value.astype(sent.dtype)
                    return 0

                lax.fori_loop(0, 2 * RING, add, 0)
                self.ring(colour, 4 + piece).start()

    def finish_ring(self):
        for colour in range(COLOURS):
            for piece in range(2, PIECES):
                self.ring(colour, piece).wait()
            at = self.place.at[ORDERS[colour][0]]
            block, land = self.block(self.total, colour, at), self.lands[0][colour]
            sent = self.block(self.sent, colour, at)

            def add(item, _):
                inner = (item // RING, item % RING)
                first, second = land[(0, *inner)], land[(1, *inner)]
                value = block[inner] + first.astype(F32) + second.astype(F32)
                block[inner] = value
                if self.sent is not self.total:
                    sent[inner] = value.astype(sent.dtype)
                return 0

            lax.fori_loop(0, RING * RING, add, 0)

    def copies(self, stage):
        for colour in range(COLOURS):
            order, (start, width) = ORDERS[colour], COLUMNS[colour]
            for step in range(1, RING):
                slot = (colour * 3 + stage) * PIECES + step - 1
                index = [slice(None)] * 3
                for axis in order[:stage]:
                    index[axis] = self.place.at[axis]
                index[order[stage]], device = self.place.peer(order[stage], step)
                yield remote(
                    self.sent.at[index[0], index[1], index[2], :, start : start + width],
                    self.lands[stage][colour].at[step - 1],
                    self.send.at[slot],
                    self.recv.at[slot],
                    device,
                )

    def start(self, stage):
        for copy in self.copies(stage):
            copy.start()

    def wait(self, stage):
        for copy in self.copies(stage):
            copy.wait()
        for colour in range(COLOURS):
            order, (start, width) = ORDERS[colour], COLUMNS[colour]
            land = self.lands[stage][colour]
            rest = sorted(order[stage + 1 :])

            def add(item, _):
                index = list(self.place.at)
                inner = [item // RING, item % RING][2 - len(rest) :]
                for axis, at in zip(rest, inner):
                    index[axis] = at
                value = self.total[
                    index[0], index[1], index[2], :, start : start + width
                ]
                for step in range(RING - 1):
                    value = value + land[(step, *inner)].astype(F32)
                at = (index[0], index[1], index[2], slice(None), slice(start, start + width))
                self.total[at] = value
                if self.sent is not self.total:
                    self.sent[at] = value.astype(self.sent.dtype)
                return 0

            lax.fori_loop(0, RING ** len(rest), add, 0)


def kernel(
    factor,
    live_total,
    q_hbm,
    c_hbm,
    r_hbm,
    counts,
    t_hbm,
    shift_s_ref,
    shift_t_ref,
    out_ref,
    big_a,
    big_b,
    t_buf,
    c_buf,
    m_hi,
    m_lo,
    q_hi,
    q_lo,
    q_bits,
    d_q,
    d_c,
    codes,
    weights,
    shift_s,
    shift_t,
    total_c,
    total_g,
    turned,
    sent_c,
    pair_land,
    slopes,
    c_left,
    c_right,
    *rest,
):
    lands_c, rest = (rest[0:3], rest[3:6], rest[6:9]), rest[9:]
    lands_g, rest = (rest[0:3], rest[3:6], rest[6:9]), rest[9:]
    (
        load,
        ag_send,
        ag_recv,
        agp_send,
        agp_recv,
        c_send,
        c_recv,
        cp_send,
        cp_recv,
        g_send,
        g_recv,
        gp_send,
        gp_recv,
        swap_send,
        swap_recv,
    ) = rest

    place = Place()
    core = place.core
    mx, my, mz = place.at

    load_r = pltpu.make_async_copy(r_hbm, big_a, load.at[0])
    load_c = pltpu.make_async_copy(
        c_hbm.at[pl.ds((place.pb // 2) * 32, 32), :], c_buf, load.at[1]
    )
    load_q = pltpu.make_async_copy(q_hbm, big_b.at[0:2], load.at[2])
    load_t = pltpu.make_async_copy(t_hbm, t_buf, load.at[3])
    load_c.start()
    load_r.start()
    load_q.start()
    load_t.start()

    barrier = pltpu.get_barrier_semaphore()
    for axis in range(3):
        for step in range(1, RING):
            _, device = place.peer(axis, step)
            pl.semaphore_signal(barrier, inc=1, device_id=device, device_id_type=MESH)
    pl.semaphore_signal(
        barrier, inc=1, device_id=place.partner(), device_id_type=MESH
    )

    load_r.wait()
    for x in range(RING):

        def split_rotation(item, _):
            value = big_a[x, item // RING, item % RING].reshape(16, -1)
            high, low = split(value)
            rows = pl.ds(pl.multiple_of(256 * x + 16 * item, 16), 16)
            m_hi[rows, :] = high
            m_lo[rows, :] = low
            return 0

        lax.fori_loop(0, RING * RING, split_rotation, 0)

    load_c.wait()
    c_high, c_low = split(c_buf[...])
    c_left[...] = jnp.concatenate([c_high, c_high, c_low], axis=0)
    c_high, c_low = split(c_buf[pl.ds(pl.multiple_of(16 * core, 16), 16), :])
    c_both = jnp.concatenate([c_high, c_low], axis=0)
    for tile in range(4):
        cols = slice(256 * tile, 256 * tile + 256)
        both = dot(c_both, m_hi[:, cols], NN)
        code = jnp.tanh(both[:16] + both[16:] + dot(c_high, m_lo[:, cols], NN))
        d_c[:, cols] = 1.0 - code * code
        codes[mx, my, mz, core, :, cols] = code.astype(BF16)

    pl.semaphore_wait(barrier, 10)
    gather = Gather(place, codes, ag_send, ag_recv, agp_send, agp_recv)
    gather.start(0)

    load_q.wait()

    def query_code(block, first):
        def split_queries(item, _):
            at = block * 32 + item
            value = big_b[at // 32, (at // 8) % 4, (at // 2) % 4, at % 2]
            high, low = split(value)
            rows = pl.ds(pl.multiple_of(16 * at, 16), 16)
            q_hi[rows, :] = high
            q_lo[rows, :] = low
            return 0

        if first == 0:
            lax.fori_loop(0, 32, split_queries, 0)
        rows = slice(512 * block, 512 * block + 512)

        def tile_code(tile, _):
            cols = pl.ds(pl.multiple_of(256 * tile, 256), 256)
            high = q_hi[rows, :]
            value = (
                dot(high, m_hi[:, cols], NN)
                + dot(q_lo[rows, :], m_hi[:, cols], NN)
                + dot(high, m_lo[:, cols], NN)
            )
            code = jnp.tanh(value)
            d_q[rows, cols] = factor * (1.0 - code * code)
            q_bits[rows, cols] = code.astype(BF16)
            return 0

        lax.fori_loop(first, first + 2, tile_code, 0)

    query_code(0, 0)
    gather.wait(0)
    gather.start(1)
    query_code(0, 2)
    gather.wait(1)
    gather.start_ring()
    for colour in range(COLOURS):
        gather.pair(colour, 0).start()
    query_code(1, 0)
    gather.relay()
    query_code(1, 2)

    shift_s[...] = jnp.broadcast_to(shift_s_ref[...], (128, 1024)).T
    shift_t[...] = jnp.broadcast_to(shift_t_ref[...], (128, 1024)).T
    load_t.wait()

    def place_of(item):
        block, half = item // 2, item % 2
        cols = pl.ds(pl.multiple_of(256 * block, 256), 256)
        rows = pl.ds(pl.multiple_of(512 * half, 512), 512)
        inner = pl.ds(pl.multiple_of(256 * (block % 4), 256), 256)
        held = big_b.at[2 * (block // 4) + half, :, :, :, :, inner]
        lane = lax.broadcasted_iota(jnp.int32, (1, 256), 1)
        limit = jnp.zeros((1, 256), jnp.int32)
        for slot in range(4):
            limit = jnp.where(lane // 64 == slot, counts[4 * block + slot], limit)
        live = jnp.where(lane % 64 < limit, 1.0 / live_total, 0.0)
        return block, rows, cols, held, live

    def teach(item, _):
        _, rows, cols, held, _ = place_of(item)
        down = shift_t[rows, :]
        target = jnp.exp(
            t_buf[rows, cols].astype(F32) - jnp.concatenate([down, down], axis=1)
        )
        held[...] = target.reshape(4, 4, 2, 16, 256)
        return 0

    lax.fori_loop(0, 16, teach, 0)
    gather.finish()

    def weigh(item, _):
        block, rows, cols, held, live = place_of(item)
        part = codes[block // 2, pl.ds(2 * (block % 2), 2)].reshape(256, -1)
        score = factor * dot(q_bits[rows, :], part, NT)
        down = shift_s[rows, :]
        student = jnp.exp(score - jnp.concatenate([down, down], axis=1))
        target = held[...].reshape(512, 256)
        weights[rows, cols] = (live * (student - target)).astype(BF16)
        return 0

    lax.fori_loop(0, 16, weigh, 0)

    def pair_c(x):
        return remote(
            sent_c.at[x],
            pair_land.at[x],
            cp_send.at[x],
            cp_recv.at[x],
            place.partner(),
        )

    for x in range(RING):
        turned[0:512, :] = weights[:, 512 * x : 512 * x + 512].T

        def corpus_grad(tile, _):
            cols = pl.ds(pl.multiple_of(256 * tile, 256), 256)
            part = dot(turned[0:512, :], q_bits[:, cols], NN)
            part = part.reshape(4, 4, 2, 16, 256)
            zero, one = part[:, :, 0], part[:, :, 1]
            total_c[x, :, :, :, cols] = lax.select(core == 0, zero, one)
            sent_c[x, :, :, :, cols] = lax.select(core == 0, one, zero).astype(BF16)
            return 0

        lax.fori_loop(0, 4, corpus_grad, 0)
        pair_c(x).start()

    def own_c(x):
        def add(item, _):
            at = (x, item // RING, item % RING)
            value = total_c[at] + pair_land[at].astype(F32)
            total_c[at] = value
            sent_c[at] = value.astype(BF16)
            return 0

        lax.fori_loop(0, RING * RING, add, 0)

    for x in range(RING):
        pair_c(x).wait()
        own_c(x)
    scatter_c = Scatter(place, total_c, sent_c, lands_c, c_send, c_recv)
    scatter_c.start_ring()

    def query_grad(item, _):
        half, tile = item // 4, item % 4
        cols = pl.ds(pl.multiple_of(256 * tile, 256), 256)
        rows = pl.ds(pl.multiple_of(512 * half, 512), 512)
        part = codes[:, :, :, :, :, cols].reshape(2048, 256)
        grad = d_q[rows, cols] * dot(weights[rows, :], part, NN)
        high, low = split(grad)
        m_hi[rows, cols] = high
        m_lo[rows, cols] = low
        return 0

    lax.fori_loop(0, 8, query_grad, 0)

    def group_cols(z_low, half):
        return pl.ds(pl.multiple_of(256 * (2 * z_low + half), 256), 256)

    def turn(half):
        for z_low in range(2):
            rows = slice(256 * z_low, 256 * z_low + 256)
            turned[rows, :] = q_hi[:, group_cols(z_low, half)].T
            rows = slice(512 + 256 * z_low, 512 + 256 * z_low + 256)
            turned[rows, :] = q_lo[:, group_cols(z_low, half)].T

    def rotation_grad(half, first):
        def tile_grad(tile, _):
            cols = pl.ds(pl.multiple_of(256 * tile, 256), 256)
            value = (
                dot(turned[0:512, :], m_hi[:, cols], NN)
                + dot(turned[512:1024, :], m_hi[:, cols], NN)
                + dot(turned[0:512, :], m_lo[:, cols], NN)
            )
            for item in range(64):
                z = 2 * (item % 2) + item // 32
                big_a[(item // 8) % 4, (item // 2) % 4, z, half, :, cols] = value[
                    8 * item : 8 * item + 8
                ]
            return 0

        lax.fori_loop(first, first + 2, tile_grad, 0)

    def pair_g(x):
        return remote(
            big_a.at[x, :, :, 1 - core],
            total_g.at[x],
            gp_send.at[x],
            gp_recv.at[x],
            place.partner(),
        )

    scatter_c.relay()
    turn(1 - core)
    rotation_grad(1 - core, 0)
    rotation_grad(1 - core, 2)
    for x in range(RING):
        pair_g(x).start()
    turn(core)
    scatter_c.finish_ring()
    scatter_c.start(1)
    rotation_grad(core, 0)
    rotation_grad(core, 2)
    scatter_c.wait(1)
    scatter_c.start(2)
    for x in range(RING):
        pair_g(x).wait()
    scatter_c.wait(2)

    slopes[core] = factor * d_c[...] * total_c[mx, my, mz]
    swap = remote(
        slopes.at[core], slopes.at[core], swap_send.at[0], swap_recv.at[0], place.partner()
    )
    swap.start()
    swap.wait()
    g_high, g_low = split(slopes[...].reshape(32, -1))
    c_right[...] = jnp.concatenate([g_high, g_low, g_high], axis=0)

    def corpus_term(tile, _):
        cols = pl.ds(pl.multiple_of(256 * tile, 256), 256)
        for z_low in range(2):
            value = dot(c_left[:, group_cols(z_low, core)], c_right[:, cols], TN)
            for item in range(32):
                at = (item // 8, (item // 2) % 4, 2 * (item % 2) + z_low)
                total_g[(*at, slice(None), cols)] = (
                    total_g[(*at, slice(None), cols)]
                    + big_a[(*at, core, slice(None), cols)]
                    + value[8 * item : 8 * item + 8]
                )
        return 0

    lax.fori_loop(0, 4, corpus_term, 0)
    scatter_g = Scatter(place, total_g, total_g, lands_g, g_send, g_recv)
    scatter_g.start_ring()
    scatter_g.relay()
    scatter_g.finish_ring()
    for stage in (1, 2):
        scatter_g.start(stage)
        scatter_g.wait(stage)
    out_ref[...] = total_g[mx, my, mz]


def per_device(queries, corpus, rotation, counts, teacher, shift_student, shift_teacher):
    rows, width = queries.shape
    slots = teacher.shape[1]
    factor = 2.5 / math.sqrt(width)

    def lands(depth, dtype):
        return [
            pltpu.VMEM((RING - 1, *(RING,) * (2 - stage), depth, COLUMNS[colour][1]), dtype)
            for stage in range(3)
            for colour in range(COLOURS)
        ]

    dma = pltpu.SemaphoreType.DMA
    any_space = pl.BlockSpec(memory_space=pl.ANY)
    vmem = pl.BlockSpec(memory_space=pltpu.VMEM)
    smem = pl.BlockSpec(memory_space=pltpu.SMEM)
    return pl.pallas_call(
        functools.partial(kernel, factor, slots // 2),
        out_shape=jax.ShapeDtypeStruct((8, width), F32),
        in_specs=[any_space, any_space, any_space, smem, any_space, vmem, vmem],
        out_specs=vmem,
        scratch_shapes=[
            pltpu.VMEM((4, 4, 4, 2, 8, width), F32),
            pltpu.VMEM((4, 4, 4, 2, 16, width), F32),
            pltpu.VMEM((rows, slots), BF16),
            pltpu.VMEM((32, width), F32),
            pltpu.VMEM((width, width), BF16),
            pltpu.VMEM((width, width), BF16),
            pltpu.VMEM((rows, width), BF16),
            pltpu.VMEM((rows, width), BF16),
            pltpu.VMEM((rows, width), BF16),
            pltpu.VMEM((rows, width), F32),
            pltpu.VMEM((16, width), F32),
            pltpu.VMEM((4, 4, 4, 2, 16, width), BF16),
            pltpu.VMEM((rows, slots), BF16),
            pltpu.VMEM((rows, 128), F32),
            pltpu.VMEM((rows, 128), F32),
            pltpu.VMEM((4, 4, 4, 16, width), F32),
            pltpu.VMEM((4, 4, 4, 8, width), F32),
            pltpu.VMEM((1024, rows), BF16),
            pltpu.VMEM((4, 4, 4, 16, width), BF16),
            pltpu.VMEM((4, 4, 4, 16, width), BF16),
            pltpu.VMEM((2, 16, width), F32),
            pltpu.VMEM((96, width), BF16),
            pltpu.VMEM((96, width), BF16),
            *lands(16, BF16),
            *lands(8, F32),
            dma((4,)),
            dma((54,)),
            dma((54,)),
            dma((12,)),
            dma((12,)),
            dma((54,)),
            dma((54,)),
            dma((4,)),
            dma((4,)),
            dma((54,)),
            dma((54,)),
            dma((4,)),
            dma((4,)),
            dma((1,)),
            dma((1,)),
        ],
        compiler_params=pltpu.CompilerParams(
            collective_id=0, has_side_effects=True, vmem_limit_bytes=67043328
        ),
    )(
        queries.reshape(2, 4, 4, 2, 16, width),
        corpus,
        rotation.reshape(4, 4, 4, 2, 8, width),
        counts,
        teacher,
        shift_student.reshape(1, rows),
        shift_teacher.reshape(1, rows),
    )


def solution(mesh):
    in_specs = (
        P(("pb", "col"), None),
        P("col", None),
        P(),
        P(),
        P(("pb", "col"), None),
        P(("pb", "col")),
        P(("pb", "col")),
    )
    return jax.shard_map(
        per_device,
        mesh=mesh,
        in_specs=in_specs,
        out_specs=P(("pb", "col"), None),
        check_vma=False,
    )
```
